768 devices in a mesh: slab: 16 (over y, x_hi), chan: 48 (over z, x_lo, core).
Axes of the slice: x: 4 (x_hi: 2, x_lo: 2; x = x_hi * 2 + x_lo), y: 8, z: 12, core: 2. Of those that a mesh axis runs over, the one named last changes fastest.
Arguments:
- volume: bfloat16 [32, 96, 64, 256], P('slab', 'chan'), may hold values from -6 to 6
- weights: bfloat16 [6912, 256], P(None, 'slab'), may hold values from -0.078125 to 0.078125
Outputs:
- conv_out: bfloat16 [32, 96, 64, 256], P('slab', 'chan')
The draws below stay inside these ranges and needn't reach their ends.
All inputs are finite; a program needn't handle non-finite values.
Results may differ from the reference program's by a relative error of at most 0.001.
Values may be sent and summed in bfloat16 or wider, within the bound.
A program may use at most 32 MiB of HBM per device.

```python
import jax
import jax.numpy as jnp
from jax import lax

C = 256
COLS = 64
DEPTH = 32
ROWS = 96


def block_scale(own_key, shape, split, least, largest):
    gain = 1.0
    for position, blocks in split:
        draws = jax.random.uniform(jax.random.fold_in(jax.random.fold_in(own_key, 6), position), (blocks,), jnp.float32, least / len(split), largest / len(split))
        gain = gain * jnp.repeat(jnp.exp(draws), shape[position] // blocks).reshape((-1,) + (1,) * (len(shape) - 1 - position))
    return gain


def scatter_about(stream_key, extent, width, limit, shards=(), kind=jnp.bfloat16):
    array = jax.random.normal(stream_key, extent, jnp.float32) * width
    if len(shards) > 0:
        array = block_scale(stream_key, extent, shards, -0.22, 0.18) * array
    return jnp.clip(array, min=-limit, max=limit).astype(kind)


def setup_inputs(seed: int = 0) -> dict:
    key_list = jax.random.split(jax.random.key(seed), 3)
    return {
        "volume": scatter_about(key_list[0], (DEPTH, ROWS, COLS, C), 1.0, 6.0, ((0, 16), (1, 48))),
        "weights": scatter_about(key_list[1], (27 * C, C), (27 * C) ** -0.5, 0.078125, ((1, 16),)),
    }


def reference(volume, weights):
    padded = jnp.pad(volume, ((1, 1), (1, 1), (1, 1), (0, 0)))
    kernel = weights.reshape(27, C, C)

    def one_plane(depth_index):
        three_planes = lax.dynamic_slice_in_dim(padded, depth_index, 3, 0)
        summed = jnp.zeros((ROWS * COLS, C), jnp.float32)
        for depth_off in range(3):
            for row_off in range(3):
                for col_off in range(3):
                    shifted = three_planes[depth_off, row_off:row_off + ROWS, col_off:col_off + COLS, :]
                    summed = summed + jnp.dot(shifted.reshape(ROWS * COLS, C), kernel[9 * depth_off + 3 * row_off + col_off], preferred_element_type=jnp.float32)
        return summed.astype(jnp.bfloat16).reshape(ROWS, COLS, C)

    return lax.map(one_plane, jnp.arange(DEPTH, dtype=jnp.int32))
```

```python
import functools

import jax
import jax.numpy as jnp
from jax import lax
from jax.experimental import pallas as pl
from jax.experimental.pallas import tpu as pltpu
from jax.sharding import PartitionSpec as P

MESH = pl.DeviceIdType.MESH
PIECES = (4, 4, 3, 3)
N = len(PIECES)
LAST = N - 1


def first_tap(i, half):
    low = sum(PIECES[:i])
    high = 13 if i == LAST else 13 + PIECES[LAST] + low
    return low + half * (high - low)


def other_taps(i):
    return PIECES[i] - 1 if i == LAST else PIECES[i]


def kernel(
    vol, w, out, *scratch
):
    a_bufs, b_bufs = scratch[:N], scratch[N : 2 * N]
    (halo, shifted, acc, own_a, own_b, swap_send, ring_send, ring_recv,
     z_send, z_recv, chip_send, chip_recv, halo_send, halo_recv, mid_sem) = scratch[2 * N :]
    s, ch = lax.axis_index("slab"), lax.axis_index("chan")
    y, xh = s // 2, s % 2
    core, xl, z = ch % 2, (ch // 2) % 2, ch // 4
    half = z % 2

    swap = (s + 1 - 2 * xh, ch + 2 - 4 * xl)
    ring = ((lax.rem(s + 2, 16), ch), (lax.rem(s + 14, 16), ch))
    zdev = ((s, lax.rem(ch + 4, 48)), (s, lax.rem(ch + 44, 48)))
    partner = (s, ch + 1 - 2 * core)
    s_up, s_dn = lax.rem(s + 1, 16), lax.rem(s + 15, 16)
    c_up, c_dn = lax.rem(ch + 1, 48), lax.rem(ch + 47, 48)
    halo_devs = (
        (s_up, ch), (s_dn, ch), (s, c_up), (s, c_dn),
        (s_up, c_up), (s_up, c_dn), (s_dn, c_up), (s_dn, c_dn),
    )

    barrier = pltpu.get_barrier_semaphore()
    greet = ring + zdev + (swap,) + halo_devs
    for dev in greet:
        pl.semaphore_signal(barrier, inc=1, device_id=dev, device_id_type=MESH)
    pl.semaphore_wait(barrier, len(greet))

    def rows(block, kind):
        return pl.ds(pl.multiple_of(block * 32 + kind * 16, 16), 16)

    def remote(src, dst, send, recv, dev):
        return pltpu.make_async_remote_copy(
            src_ref=src, dst_ref=dst, send_sem=send, recv_sem=recv,
            device_id=dev, device_id_type=MESH,
        )

    def lanes(start, taps):
        return pl.ds(pl.multiple_of(start * 256, 256), taps * 256)

    mine = rows(y, core)
    pltpu.make_async_copy(vol, halo.at[1:3, 1:3], mid_sem).start()

    def own_src(i, which):
        if which == 0:
            return w.at[:, lanes(first_tap(i, half), PIECES[i])]
        start = first_tap(i, 1 - half) + ((1 - half) if i == LAST else 0)
        return w.at[:, lanes(start, other_taps(i))]

    @pl.when(core == xh)
    def _():
        for which, bufs, sem in ((0, a_bufs, own_a), (1, b_bufs, own_b)):
            for i in range(N):
                src, dst = own_src(i, which), bufs[i].at[mine, :]
                remote(src, dst, swap_send.at[which, i], sem.at[i], swap).start()
                pltpu.make_async_copy(src, dst, sem.at[i]).start()

    sends = (
        (vol.at[1:2], halo.at[0:1, 1:3]),
        (vol.at[0:1], halo.at[3:4, 1:3]),
        (vol.at[:, 1:2], halo.at[1:3, 0:1]),
        (vol.at[:, 0:1], halo.at[1:3, 3:4]),
        (vol.at[1:2, 1:2], halo.at[0:1, 0:1]),
        (vol.at[1:2, 0:1], halo.at[0:1, 3:4]),
        (vol.at[0:1, 1:2], halo.at[3:4, 0:1]),
        (vol.at[0:1, 0:1], halo.at[3:4, 3:4]),
    )
    halo_copies = [
        remote(src, dst, halo_send, halo_recv.at[n], halo_devs[n])
        for n, (src, dst) in enumerate(sends)
    ]
    for copy in halo_copies:
        copy.start()

    def hops(d, k, i):
        return k < 3 or (k == 3 and (i % 2 == 0) == (d == 0))

    def block_of(d, k):
        return lax.rem(y + (7 - k if d == 0 else 1 + k), 8)

    def ring_copy(d, k, i):
        ref = a_bufs[i].at[rows(block_of(d, k - 1), core), :]
        return remote(ref, ref, ring_send.at[d, i], ring_recv.at[d, k, i], ring[d])

    def ring_wait(d, k, i):
        ref = a_bufs[i].at[rows(block_of(d, k), core), :]
        remote(ref, ref, ring_send.at[d, i], ring_recv.at[d, k, i], ring[d]).wait_recv()

    def z_copy(d, k, i):
        block = rows(block_of(d, k), core)
        if i == LAST:
            src = a_bufs[i].at[block, lanes(half, other_taps(i))]
        else:
            src = a_bufs[i].at[block, :]
        return remote(src, b_bufs[i].at[block, :], z_send.at[d, i], z_recv.at[d, k, i], zdev[d])

    def z_wait(d, k, i):
        ref = b_bufs[i].at[rows(block_of(d, k), core), :]
        remote(ref, ref, z_send.at[d, i], z_recv.at[d, k, i], zdev[d]).wait_recv()

    def chip_copy(which, block, i):
        ref = (a_bufs, b_bufs)[which][i].at[rows(block, core), :]
        return remote(ref, ref, chip_send.at[which, i], chip_recv.at[which, i], partner)

    def ring_events(k, i):
        for d in (0, 1):
            if hops(d, k, i):
                ring_wait(d, k, i)
                if hops(d, k + 1, i):
                    ring_copy(d, k + 1, i).start()
                z_copy(d, k, i).start()
                chip_copy(0, block_of(d, k), i).start()

    def z_events(k, i):
        for d in (0, 1):
            if hops(d, k, i):
                z_wait(d, k, i)
                chip_copy(1, block_of(d, k), i).start()

    def spread(d):
        for r in range(4):
            there = None
            if d == 0:
                there = s > 0
            if d == 3:
                there = s < 15
            if r == 0:
                there = (ch > 0) if there is None else there & (ch > 0)
            if r == 3:
                there = (ch < 47) if there is None else there & (ch < 47)
            plane = halo[d, r].astype(jnp.float32)
            if there is not None:
                plane = jnp.where(there, plane, 0.0)
            at = lax.broadcasted_iota(jnp.int32, plane.shape, 0)
            low = jnp.where(at == 0, 0.0, pltpu.roll(plane, 1, 0))
            high = jnp.where(at == 63, 0.0, pltpu.roll(plane, 63, 0))
            shifted[0, d, r] = low.astype(jnp.bfloat16)
            shifted[1, d, r] = plane.astype(jnp.bfloat16)
            shifted[2, d, r] = high.astype(jnp.bfloat16)

    def multiply(which, i):
        bufs = (a_bufs, b_bufs)[which]
        pltpu.make_async_copy(
            bufs[i].at[0:128, :], bufs[i].at[0:128, :], chip_recv.at[which, i]
        ).wait()
        if which == 0:
            start, count = first_tap(i, half), PIECES[i]
        else:
            count = other_taps(i)
            start = first_tap(i, 1 - half) + ((1 - half) if i == LAST else 0)
        taps = []
        for j in range(count):
            t = start + j
            a, b, e = t // 9, (t // 3) % 3, t % 3
            taps.append(
                jnp.concatenate(
                    [shifted[e, a + dd, b + rr] for dd in (0, 1) for rr in (0, 1)], axis=0
                )
            )
        left = jnp.concatenate(taps, axis=1)
        part = lax.dot_general(
            left, bufs[i][...], (((1,), (1,)), ((), ())), preferred_element_type=jnp.float32
        )
        if which == 0 and i == 0:
            acc[...] = part
        else:
            acc[...] += part

    for i in range(N):
        ref = a_bufs[i].at[mine, :]
        pltpu.make_async_copy(ref, ref, own_a.at[i]).wait()
        ring_copy(0, 0, i).start()
        ring_copy(1, 0, i).start()
        chip_copy(0, y, i).start()
    for k in range(4):
        if k == 2:
            for n, copy in enumerate(halo_copies):
                copy.wait_recv()
            pltpu.make_async_copy(vol, halo.at[1:3, 1:3], mid_sem).wait()
            for i in range(N):
                ref = b_bufs[i].at[mine, :]
                pltpu.make_async_copy(ref, ref, own_b.at[i]).wait()
                chip_copy(1, y, i).start()
        for i in range(N):
            ring_events(k, i)
            if k > 0:
                z_events(k - 1, i)
            if k == 2:
                for d in range(4 * i // N, 4 * (i + 1) // N):
                    spread(d)
    for i in range(N):
        multiply(0, i)
        z_events(3, i)
    for i in range(N):
        multiply(1, i)
    out[...] = acc[...].astype(jnp.bfloat16).reshape(out.shape)

    def drain(ref, sem):
        pltpu.make_async_copy(ref, ref, sem).wait()

    @pl.when(core == xh)
    def _():
        for which, bufs in ((0, a_bufs), (1, b_bufs)):
            for i in range(N):
                drain(bufs[i].at[0:16, :], swap_send.at[which, i])

    for i in range(N):
        for d in (0, 1):
            count = 3 + hops(d, 3, i)
            drain(a_bufs[i].at[0 : 16 * count, :], ring_send.at[d, i])
            drain(b_bufs[i].at[0 : 16 * count, :], z_send.at[d, i])
        drain(a_bufs[i].at[0:128, :], chip_send.at[0, i])
        drain(b_bufs[i].at[0:128, :], chip_send.at[1, i])
    drain(halo.at[0:3], halo_send)


def solution(mesh):
    def local(volume, weights):
        dma = pltpu.SemaphoreType.DMA
        return pl.pallas_call(
            kernel,
            out_shape=jax.ShapeDtypeStruct(volume.shape, jnp.bfloat16),
            in_specs=[pl.BlockSpec(memory_space=pl.ANY)] * 2,
            out_specs=pl.BlockSpec(memory_space=pltpu.VMEM),
            scratch_shapes=[pltpu.VMEM((256, 256 * n), jnp.bfloat16) for n in PIECES]
            + [pltpu.VMEM((256, 256 * other_taps(i)), jnp.bfloat16) for i in range(N)]
            + [
                pltpu.VMEM((4, 4, 64, 256), jnp.bfloat16),
                pltpu.VMEM((3, 4, 4, 64, 256), jnp.bfloat16),
                pltpu.VMEM((256, 256), jnp.float32),
                dma((N,)),
                dma((N,)),
                dma((2, N)),
                dma((2, N)),
                dma((2, 4, N)),
                dma((2, N)),
                dma((2, 4, N)),
                dma((2, N)),
                dma((2, N)),
                dma(()),
                dma((8,)),
                dma(()),
            ],
            compiler_params=pltpu.CompilerParams(collective_id=0, has_side_effects=True),
            name="conv_gather",
        )(volume, weights.T)

    return jax.shard_map(
        local,
        mesh=mesh,
        in_specs=(P("slab", "chan", None, None), P(None, "slab")),
        out_specs=P("slab", "chan", None, None),
        check_vma=False,
    )
```

```python
import jax
import jax.numpy as jnp
from jax import lax
from jax.experimental import pallas as pl
from jax.experimental.pallas import tpu as pltpu
from jax.sharding import PartitionSpec as P

MESH = pl.DeviceIdType.MESH
PIECES = (2, 2, 2, 2, 2, 2, 2)
N = len(PIECES)
LAST = N - 1
EDGE = (4, 5)
ZS = 12


def first_tap(i, half):
    low = sum(PIECES[:i])
    high = 13 if i == LAST else 13 + PIECES[LAST] + low
    return low + half * (high - low)


def other_taps(i):
    return PIECES[i] - 1 if i == LAST else PIECES[i]


def hops(d, k, i):
    return k < 3 or (k == 3 and (i % 2 == 0) == (d == 0))


def count(d, i):
    return 3 + hops(d, 3, i)


def kernel(vol, w, out, *scratch):
    a_bufs, b_bufs = scratch[:N], scratch[N : 2 * N]
    (halo, shifted, acc, own, swap_send, ring_send, ring_recv, z_send, z_recv, edge_send,
     chip_send, chip_recv, halo_send, halo_recv, mid_sem, near_sem, far_sem) = scratch[2 * N :]
    bufs = (a_bufs, b_bufs)
    s, ch = lax.axis_index("slab"), lax.axis_index("chan")
    y, xh = s // 2, s % 2
    core, xl, z = ch % 2, (ch // 2) % 2, ch // 4
    half = z % 2
    at_edge = (z == 0) | (z == ZS - 1)

    swap = (s + 1 - 2 * xh, ch + 2 - 4 * xl)
    across = (s, ch + 2 - 4 * xl)
    ring = ((lax.rem(s + 2, 16), ch), (lax.rem(s + 14, 16), ch))
    zdev = ((s, jnp.minimum(ch + 4, 47)), (s, jnp.maximum(ch - 4, 0)))
    has_z = (z < ZS - 1, z > 0)
    partner = (s, ch + 1 - 2 * core)
    depth_dev = ((lax.rem(s + 1, 16), ch), (lax.rem(s + 15, 16), ch))
    row_dev = ((s, jnp.minimum(ch + 1, 47)), (s, jnp.maximum(ch - 1, 0)))
    has_row = (ch < 47, ch > 0)
    n_near = 5 + jnp.where(z < ZS - 1, 1, 0) + jnp.where(z > 0, 1, 0)

    def greet(sem):
        for dev in ring + (swap, across, partner):
            pl.semaphore_signal(sem, inc=1, device_id=dev, device_id_type=MESH)
        for d in (0, 1):

            @pl.when(has_z[d])
            def _():
                pl.semaphore_signal(sem, inc=1, device_id=zdev[d], device_id_type=MESH)

    barrier = pltpu.get_barrier_semaphore()
    greet(barrier)
    pl.semaphore_wait(barrier, n_near)

    def rows(block, kind):
        return pl.ds(pl.multiple_of(block * 32 + kind * 16, 16), 16)

    def remote(src, dst, send, recv, dev):
        return pltpu.make_async_remote_copy(
            src_ref=src, dst_ref=dst, send_sem=send, recv_sem=recv,
            device_id=dev, device_id_type=MESH,
        )

    def lanes(start, taps):
        return pl.ds(pl.multiple_of(start * 256, 256), taps * 256)

    def taps_of(which, i):
        if which == 0:
            return first_tap(i, half), PIECES[i]
        return first_tap(i, 1 - half) + ((1 - half) if i == LAST else 0), other_taps(i)

    def land(sem, ref):
        pltpu.make_async_copy(ref, ref, sem).wait()

    def block_of(d, k):
        return lax.rem(y + (7 - k if d == 0 else 1 + k), 8)

    def ring_copy(d, k, i, src=None):
        ref = a_bufs[i].at[rows(block_of(d, k - 1), core), :]
        return remote(ref if src is None else src, ref, ring_send.at[d, i], ring_recv.at[d, k, i], ring[d])

    def edge_copy(d, k, i, src=None):
        ref = b_bufs[i].at[rows(block_of(d, k - 1), core), :]
        return remote(ref if src is None else src, ref, edge_send.at[d, i], z_recv.at[d, k, i], ring[d])

    def z_copy(d, k, i, to):
        block = rows(block_of(d, k), core)
        if i == LAST:
            src = a_bufs[i].at[block, lanes(half, other_taps(i))]
        else:
            src = a_bufs[i].at[block, :]
        return remote(src, b_bufs[i].at[block, :], z_send.at[to, i], z_recv.at[d, k, i], zdev[to])

    def chip_copy(which, block, i, src=None):
        ref = bufs[which][i].at[rows(block, core), :]
        return remote(
            ref if src is None else src, ref, chip_send.at[which, i], chip_recv.at[which, i], partner
        )

    mine = rows(y, core)

    def own_src(which, i):
        start, taps = taps_of(which, i)
        return w.at[:, lanes(start, taps)]

    greet(near_sem)

    @pl.when(core == xh)
    def _():
        for i in range(N):
            src = own_src(0, i)
            remote(src, a_bufs[i].at[mine, :], swap_send.at[0, i], own.at[0, i], swap).start()
            for d in (0, 1):
                ring_copy(d, 0, i, src).start()
        for i in range(N):
            src = own_src(1, i)
            remote(src, b_bufs[i].at[mine, :], swap_send.at[1, i], own.at[1, i], swap).start()
            if i in EDGE:

                @pl.when(at_edge)
                def _():
                    for d in (0, 1):
                        edge_copy(d, 0, i, src).start()

        for which in (0, 1):
            for i in range(N):
                src = own_src(which, i)
                chip_copy(which, y, i, src).start()
                pltpu.make_async_copy(src, bufs[which][i].at[mine, :], own.at[which, i]).start()

    pltpu.make_async_copy(vol, halo.at[1:3, 1:3], mid_sem).start()
    pl.semaphore_wait(near_sem, n_near)
    greet(far_sem)
    pl.semaphore_wait(far_sem, n_near)

    depth_copies = [
        remote(vol.at[1:2], halo.at[0:1, 1:3], halo_send.at[0], halo_recv.at[0], depth_dev[0]),
        remote(vol.at[0:1], halo.at[3:4, 1:3], halo_send.at[1], halo_recv.at[1], depth_dev[1]),
    ]
    row_copies = [
        remote(halo.at[:, 2:3], halo.at[:, 0:1], halo_send.at[2], halo_recv.at[2], row_dev[0]),
        remote(halo.at[:, 1:2], halo.at[:, 3:4], halo_send.at[3], halo_recv.at[3], row_dev[1]),
    ]
    for copy in depth_copies:
        copy.start()

    @pl.when(core != xh)
    def _():
        for i in range(N):
            land(own.at[0, i], a_bufs[i].at[mine, :])
            for d in (0, 1):
                ring_copy(d, 0, i, a_bufs[i].at[mine, :]).start()
            chip_copy(0, y, i).start()

    def ring_events(k, i):
        for d in (0, 1):
            if not hops(d, k, i):
                continue
            ref = a_bufs[i].at[rows(block_of(d, k), core), :]
            remote(ref, ref, ring_send.at[d, i], ring_recv.at[d, k, i], ring[d]).wait_recv()
            if hops(d, k + 1, i):
                ring_copy(d, k + 1, i).start()
            toward = (z == ZS - 2) if d == 0 else (z == 1)
            away = (z == 1) if d == 0 else (z == ZS - 2)
            plain = has_z[d] & jnp.logical_not(toward) if i in EDGE else has_z[d]

            @pl.when(plain)
            def _():
                z_copy(d, k, i, d).start()

            if i not in EDGE:

                @pl.when(away)
                def _():
                    z_copy(d, k, i, 1 - d).start()

            chip_copy(0, block_of(d, k), i).start()

    def z_events(k, i):
        for d in (0, 1):
            if not hops(d, k, i):
                continue
            ref = b_bufs[i].at[rows(block_of(d, k), core), :]
            remote(ref, ref, z_send.at[d, i], z_recv.at[d, k, i], zdev[d]).wait_recv()
            if i in EDGE and hops(d, k + 1, i):

                @pl.when(at_edge)
                def _():
                    edge_copy(d, k + 1, i).start()

            chip_copy(1, block_of(d, k), i).start()

    def spread(d):
        for r in range(4):
            there = []
            if d == 0:
                there.append(s > 0)
            if d == 3:
                there.append(s < 15)
            if r == 0:
                there.append(ch > 0)
            if r == 3:
                there.append(ch < 47)
            plane = halo[d, r].astype(jnp.float32)
            for cond in there:
                plane = jnp.where(cond, plane, 0.0)
            at = lax.broadcasted_iota(jnp.int32, plane.shape, 0)
            low = jnp.where(at == 0, 0.0, pltpu.roll(plane, 1, 0))
            high = jnp.where(at == 63, 0.0, pltpu.roll(plane, 63, 0))
            shifted[0, d, r] = low.astype(jnp.bfloat16)
            shifted[1, d, r] = plane.astype(jnp.bfloat16)
            shifted[2, d, r] = high.astype(jnp.bfloat16)

    def multiply(which, i):
        buf = bufs[which][i]
        land(chip_recv.at[which, i], buf.at[0:128, :])
        start, number = taps_of(which, i)
        taps = []
        for j in range(number):
            t = start + j
            a, b, e = t // 9, (t // 3) % 3, t % 3
            taps.append(
                jnp.concatenate(
                    [shifted[e, a + dd, b + rr] for dd in (0, 1) for rr in (0, 1)], axis=0
                )
            )
        left = jnp.concatenate(taps, axis=1)
        part = lax.dot_general(
            left, buf[...], (((1,), (1,)), ((), ())), preferred_element_type=jnp.float32
        )
        if which == 0 and i == 0:
            acc[...] = part
        else:
            acc[...] += part

    for k in range(4):
        for i in range(N):
            ring_events(k, i)
            if k > 0:
                z_events(k - 1, i)
            if k == 3 and i < 4:
                spread(i)
        if k == 0:

            @pl.when(core != xh)
            def _():
                for i in range(N):
                    land(own.at[1, i], b_bufs[i].at[mine, :])
                    chip_copy(1, y, i).start()
                    if i in EDGE:

                        @pl.when(at_edge)
                        def _():
                            for d in (0, 1):
                                edge_copy(d, 0, i, b_bufs[i].at[mine, :]).start()

        if k == 1:
            for copy in depth_copies:
                copy.wait_recv()
            land(mid_sem, halo.at[1:3, 1:3])
            for d in (0, 1):

                @pl.when(has_row[d])
                def _():
                    row_copies[d].start()

        if k == 2:
            for d in (0, 1):

                @pl.when(has_row[1 - d])
                def _():
                    row_copies[d].wait_recv()

            @pl.when(core == xh)
            def _():
                for which in (0, 1):
                    for i in range(N):
                        land(own.at[which, i], bufs[which][i].at[mine, :])

    for i in range(N):
        multiply(0, i)
        z_events(3, i)
    for i in range(N):
        multiply(1, i)
    out[...] = acc[...].astype(jnp.bfloat16).reshape(out.shape)

    def left(buf, blocks, sem):
        land(sem, buf.at[0 : 16 * blocks, :])

    @pl.when(core == xh)
    def _():
        for which in (0, 1):
            for i in range(N):
                left(bufs[which][i], 1, swap_send.at[which, i])

    for i in range(N):
        both = count(0, i) + count(1, i)
        for d in (0, 1):
            left(a_bufs[i], count(d, i), ring_send.at[d, i])
            toward = (z == ZS - 2) if d == 0 else (z == 1)

            @pl.when(has_z[d] & jnp.logical_not(toward))
            def _():
                left(b_bufs[i], count(d, i), z_send.at[d, i])

            if i not in EDGE:

                @pl.when(toward)
                def _():
                    left(b_bufs[i], both, z_send.at[d, i])

            else:

                @pl.when(at_edge)
                def _():
                    left(b_bufs[i], count(d, i), edge_send.at[d, i])

        for which in (0, 1):
            left(bufs[which][i], 8, chip_send.at[which, i])
    for copy in depth_copies:
        copy.wait_send()
    for d in (0, 1):

        @pl.when(has_row[d])
        def _():
            row_copies[d].wait_send()


def solution(mesh):
    def local(volume, weights):
        dma, regular = pltpu.SemaphoreType.DMA, pltpu.SemaphoreType.REGULAR
        return pl.pallas_call(
            kernel,
            out_shape=jax.ShapeDtypeStruct(volume.shape, jnp.bfloat16),
            in_specs=[pl.BlockSpec(memory_space=pl.ANY)] * 2,
            out_specs=pl.BlockSpec(memory_space=pltpu.VMEM),
            scratch_shapes=[pltpu.VMEM((256, 256 * n), jnp.bfloat16) for n in PIECES]
            + [pltpu.VMEM((256, 256 * other_taps(i)), jnp.bfloat16) for i in range(N)]
            + [
                pltpu.VMEM((4, 4, 64, 256), jnp.bfloat16),
                pltpu.VMEM((3, 4, 4, 64, 256), jnp.bfloat16),
                pltpu.VMEM((256, 256), jnp.float32),
                dma((2, N)),
                dma((2, N)),
                dma((2, N)),
                dma((2, 4, N)),
                dma((2, N)),
                dma((2, 4, N)),
                dma((2, N)),
                dma((2, N)),
                dma((2, N)),
                dma((4,)),
                dma((4,)),
                dma(()),
                regular,
                regular,
            ],
            compiler_params=pltpu.CompilerParams(collective_id=0, has_side_effects=True),
            name="conv_gather",
        )(volume, weights.T)

    return jax.shard_map(
        local,
        mesh=mesh,
        in_specs=(P("slab", "chan", None, None), P(None, "slab")),
        out_specs=P("slab", "chan", None, None),
        check_vma=False,
    )
```

```python
import jax
import jax.numpy as jnp
from jax import lax
from jax.experimental import pallas as pl
from jax.experimental.pallas import tpu as pltpu
from jax.sharding import PartitionSpec as P

MESH = pl.DeviceIdType.MESH
PIECES = (7, 7)
N = len(PIECES)
LAST = N - 1
ZS = 12
LAG = 2


def first_tap(i, half):
    low = sum(PIECES[:i])
    high = 13 if i == LAST else 13 + PIECES[LAST] + low
    return low + half * (high - low)


def other_taps(i):
    return PIECES[i] - 1 if i == LAST else PIECES[i]


def hops(d, k, i):
    return k < 3 or (k == 3 and (i % 2 == 0) == (d == 0))


def count(d, i):
    return 3 + hops(d, 3, i)


def kernel(vol, w, out, *scratch):
    a_bufs, b_bufs = scratch[:N], scratch[N : 2 * N]
    (halo, shifted, acc, own, swap_send, ring_send, ring_recv, z_send, z_recv,
     chip_send, chip_recv, halo_send, halo_recv, mid_sem, near_sem, far_sem, late_sem) = scratch[2 * N :]
    bufs = (a_bufs, b_bufs)
    s, ch = lax.axis_index("slab"), lax.axis_index("chan")
    y, xh = s // 2, s % 2
    core, xl, z = ch % 2, (ch // 2) % 2, ch // 4
    half = z % 2
    is_late = (s == 0) & (ch == 0)
    is_host = (s == 0) & (ch == 1)
    meets_late = (s == 1) & (ch == 0)
    active = jnp.logical_not(is_late)
    plain = jnp.logical_not((s == 0) & (ch < 2))
    here = core == xh

    def host(dev):
        return dev[0], jnp.where((dev[0] == 0) & (dev[1] == 0), 1, dev[1])

    def seat(kind):
        return ch - core + kind

    def ring_dev(d, kind):
        return host((lax.rem(s + (2 if d == 0 else 14), 16), seat(kind)))

    def swap_dev(kind):
        return host((s + 1 - 2 * xh, seat(kind) + 2 - 4 * xl))

    def z_dev(d, kind):
        c = seat(kind)
        return host((s, jnp.minimum(c + 4, 47) if d == 0 else jnp.maximum(c - 4, 0)))

    def devices(kind):
        return (
            (ring_dev(0, kind), ring_dev(1, kind)), swap_dev(kind),
            (z_dev(0, kind), z_dev(1, kind)), host((s, seat(kind) + 2 - 4 * xl)),
        )

    own_devices, zero_devices = devices(core), devices(0)

    def ring_of(kind):
        return (own_devices if kind is core else zero_devices)[0]

    def swap_of(kind):
        return (own_devices if kind is core else zero_devices)[1]

    def z_of(kind):
        return (own_devices if kind is core else zero_devices)[2]

    def across_of(kind):
        return (own_devices if kind is core else zero_devices)[3]

    partner = (s, ch + 1 - 2 * core)
    has_z = (z < ZS - 1, z > 0)
    depth_dev = ((jnp.minimum(s + 1, 15), ch), (jnp.maximum(s - 1, 0), ch))
    has_depth = (s < 15, s > 0)
    row_dev = ((s, jnp.minimum(ch + 1, 47)), (s, jnp.maximum(ch - 1, 0)))
    has_row = (ch < 47, ch > 0)

    def signal(sem, dev):
        pl.semaphore_signal(sem, inc=1, device_id=dev, device_id_type=MESH)

    def greet_as(sem, kind):
        for d in (0, 1):
            signal(sem, ring_of(kind)[d])
        signal(sem, swap_of(kind))
        signal(sem, across_of(kind))

    def greet(sem):
        greet_as(sem, core)

        @pl.when(plain)
        def _():
            signal(sem, partner)

        @pl.when(is_host)
        def _():
            greet_as(sem, 0)

    n_plane = jnp.where(is_host, 8, 5)
    n_z = has_z[0].astype(jnp.int32) + has_z[1].astype(jnp.int32)

    barrier = pltpu.get_barrier_semaphore()

    @pl.when(active)
    def _():
        greet(barrier)

    def greet_z(kind):
        for d in (0, 1):

            @pl.when(has_z[d])
            def _():
                signal(barrier, z_of(kind)[d])

    @pl.when(active)
    def _():
        greet_z(core)

    @pl.when(is_host)
    def _():
        greet_z(0)

    @pl.when(is_host | meets_late)
    def _():
        signal(barrier, (0, 0))

    pl.semaphore_wait(barrier, jnp.where(is_late, 2, n_plane + n_z * jnp.where(is_host, 2, 1)))

    @pl.when(is_late)
    def _():
        signal(late_sem, (0, 1))
        signal(late_sem, (1, 0))

    def remote(src, dst, send, recv, dev):
        return pltpu.make_async_remote_copy(
            src_ref=src, dst_ref=dst, send_sem=send, recv_sem=recv,
            device_id=dev, device_id_type=MESH,
        )

    def lanes(start, taps):
        return pl.ds(pl.multiple_of(start * 256, 256), taps * 256)

    def taps_of(which, i):
        if which == 0:
            return first_tap(i, half), PIECES[i]
        return first_tap(i, 1 - half) + ((1 - half) if i == LAST else 0), other_taps(i)

    def land(sem, ref):
        pltpu.make_async_copy(ref, ref, sem).wait()

    blocks = [[lax.rem(y + (7 - k if d == 0 else 1 + k), 8) for k in range(4)] for d in (0, 1)]

    def block_of(d, k):
        return y if k < 0 else blocks[d][k]

    def ring_copy(d, k, i, kind, src=None):
        ref = a_bufs[i].at[block_of(d, k - 1), kind]
        return remote(
            ref if src is None else src, ref,
            ring_send.at[kind, d, i], ring_recv.at[kind, d, k, i], ring_of(kind)[d],
        )

    def z_copy(d, k, i, to, kind):
        block = block_of(d, k)
        if i == LAST:
            src = a_bufs[i].at[block, kind, :, lanes(half, other_taps(i))]
        else:
            src = a_bufs[i].at[block, kind]
        return remote(
            src, b_bufs[i].at[block, kind],
            z_send.at[kind, to, i], z_recv.at[kind, d, k, i], z_of(kind)[to],
        )

    def chip_give(which, i):
        @pl.when(plain)
        def _():
            ref = bufs[which][i].at[:, core]
            remote(ref, ref, chip_send.at[which, i], chip_recv.at[which, i], partner).start()

    def host_give(which, i, early):
        for part in ((slice(0, 4), slice(5, 8)) if early else (slice(4, 5),)):
            ref = bufs[which][i].at[part]
            remote(ref, ref, chip_send.at[which, i], chip_recv.at[which, i], partner).start()

    def own_src(which, i):
        start, taps = taps_of(which, i)
        return w.at[:, lanes(start, taps)]

    def give_a(kind):
        for i in range(N):
            src, mine = own_src(0, i), a_bufs[i].at[y, kind]
            remote(src, mine, swap_send.at[kind, 0, i], own.at[kind, 0, i], swap_of(kind)).start()
            for d in (0, 1):
                ring_copy(d, 0, i, kind, src).start()

    def give_b(kind):
        for i in range(N):
            src, mine = own_src(1, i), b_bufs[i].at[y, kind]
            remote(src, mine, swap_send.at[kind, 1, i], own.at[kind, 1, i], swap_of(kind)).start()

    def keep(kind):
        for which in (0, 1):
            for i in range(N):
                src, mine = own_src(which, i), bufs[which][i].at[y, kind]
                pltpu.make_async_copy(src, mine, own.at[kind, which, i]).start()

    def ring_events(k, i, kind):
        for d in (0, 1):
            if not hops(d, k, i):
                continue
            land(ring_recv.at[kind, d, k, i], a_bufs[i].at[block_of(d, k), kind])
            if hops(d, k + 1, i):
                ring_copy(d, k + 1, i, kind).start()
            away = (z == 1) if d == 0 else (z == ZS - 2)

            @pl.when(has_z[d])
            def _():
                z_copy(d, k, i, d, kind).start()

            @pl.when(away)
            def _():
                z_copy(d, k, i, 1 - d, kind).start()

    def z_events(k, i, kind):
        for d in (0, 1):
            if not hops(d, k, i):
                continue
            land(z_recv.at[kind, d, k, i], b_bufs[i].at[block_of(d, k), kind])

    depth_copies = [
        remote(vol.at[1:2], halo.at[0:1, 1:3], halo_send.at[0], halo_recv.at[0], depth_dev[0]),
        remote(vol.at[0:1], halo.at[3:4, 1:3], halo_send.at[1], halo_recv.at[1], depth_dev[1]),
    ]
    row_copies = [
        remote(halo.at[:, 2:3], halo.at[:, 0:1], halo_send.at[2], halo_recv.at[2], row_dev[0]),
        remote(halo.at[:, 1:2], halo.at[:, 3:4], halo_send.at[3], halo_recv.at[3], row_dev[1]),
    ]

    def halo_rows():
        for d in (0, 1):

            @pl.when(has_depth[1 - d])
            def _():
                depth_copies[d].wait_recv()

        land(mid_sem, halo.at[1:3, 1:3])
        for d in (0, 1):
            wanted = has_row[d] if d == 0 else has_row[d] & jnp.logical_not(is_host)

            @pl.when(wanted)
            def _():
                row_copies[d].start()

    def spread(d):
        for r in range(4):
            there = []
            if d == 0:
                there.append(s > 0)
            if d == 3:
                there.append(s < 15)
            if r == 0:
                there.append(ch > 0)
            if r == 3:
                there.append(ch < 47)
            x = halo[d, r].astype(jnp.float32)
            for cond in there:
                x = jnp.where(cond, x, 0.0)
            at = lax.broadcasted_iota(jnp.int32, x.shape, 0)
            low = jnp.where(at == 0, 0.0, pltpu.roll(x, 1, 0))
            high = jnp.where(at == 63, 0.0, pltpu.roll(x, 63, 0))
            shifted[0, d, r] = low.astype(jnp.bfloat16)
            shifted[1, d, r] = x.astype(jnp.bfloat16)
            shifted[2, d, r] = high.astype(jnp.bfloat16)

    def multiply(which, i):
        buf = bufs[which][i]

        @pl.when(plain)
        def _():
            land(chip_recv.at[which, i], buf.at[:, core])

        @pl.when(is_late)
        def _():
            land(chip_recv.at[which, i], buf)

        start, number = taps_of(which, i)
        taps = []
        for j in range(number):
            t = start + j
            a, b, e = t // 9, (t // 3) % 3, t % 3
            taps.append(
                jnp.concatenate(
                    [shifted[e, a + dd, b + rr] for dd in (0, 1) for rr in (0, 1)], axis=0
                )
            )
        left = jnp.concatenate(taps, axis=1)
        part = lax.dot_general(
            left, buf[...].reshape(256, 256 * number), (((1,), (1,)), ((), ())), preferred_element_type=jnp.float32
        )
        if which == 0 and i == 0:
            acc[...] = part
        else:
            acc[...] += part

    pltpu.make_async_copy(vol, halo.at[1:3, 1:3], mid_sem).start()

    @pl.when(is_late)
    def _():
        depth_copies[0].start()
        halo_rows()

    @pl.when(active)
    def _():
        greet(near_sem)

        @pl.when(is_host)
        def _():
            give_a(0)

        @pl.when(here)
        def _():
            give_a(core)
            give_b(core)
            keep(core)

        @pl.when(is_host)
        def _():
            give_b(0)
            keep(0)

        @pl.when(jnp.logical_not(here))
        def _():
            for i in range(N):
                land(own.at[core, 0, i], a_bufs[i].at[y, core])
                for d in (0, 1):
                    ring_copy(d, 0, i, core, a_bufs[i].at[y, core]).start()

        pl.semaphore_wait(near_sem, n_plane)
        greet(far_sem)
        for k in range(4):
            for i in range(N):
                ring_events(k, i, core)

                @pl.when(is_host)
                def _():
                    ring_events(k, i, 0)

                if k == 3:

                    @pl.when(plain)
                    def _():
                        chip_give(0, i)

                if k >= LAG:
                    z_events(k - LAG, i, core)
            if k == 0:
                pl.semaphore_wait(far_sem, n_plane)
                for d in (0, 1):
                    wanted = has_depth[d] if d == 0 else has_depth[d] & jnp.logical_not(meets_late)

                    @pl.when(wanted)
                    def _():
                        depth_copies[d].start()

                @pl.when(here)
                def _():
                    for which in (0, 1):
                        for i in range(N):
                            land(own.at[core, which, i], bufs[which][i].at[y, core])

                @pl.when(jnp.logical_not(here))
                def _():
                    for i in range(N):
                        land(own.at[core, 1, i], b_bufs[i].at[y, core])

            if k == 2:

                @pl.when(meets_late)
                def _():
                    pl.semaphore_wait(late_sem, 1)
                    depth_copies[1].start()

                @pl.when(jnp.logical_not(meets_late))
                def _():
                    halo_rows()

                @pl.when(is_host)
                def _():
                    pl.semaphore_wait(late_sem, 1)
                    row_copies[1].start()
                    for which in (0, 1):
                        for i in range(N):
                            land(own.at[0, which, i], bufs[which][i].at[y, 0])
                    for i in range(N):
                        host_give(0, i, True)

        @pl.when(meets_late)
        def _():
            halo_rows()

        @pl.when(is_host)
        def _():
            for i in range(N):
                host_give(0, i, False)

        for k in range(4 - LAG, 3):
            for i in range(N):
                z_events(k, i, core)

        @pl.when(is_host)
        def _():
            for i in range(N):
                for k in range(3):
                    z_events(k, i, 0)
                host_give(1, i, True)

    for d in (0, 1):

        @pl.when(has_row[1 - d])
        def _():
            row_copies[d].wait_recv()

    for d in range(4):
        spread(d)
    for i in range(N):
        multiply(0, i)

        @pl.when(active)
        def _():
            z_events(3, i, core)

        @pl.when(is_host)
        def _():
            z_events(3, i, 0)
            host_give(1, i, False)

        chip_give(1, i)

    for i in range(N):
        multiply(1, i)
    out[...] = acc[...].astype(jnp.bfloat16).reshape(out.shape)

    def left(buf, blocks, sem):
        land(sem, buf if blocks == 16 else buf.at[0:blocks, 0])

    def gone(kind):
        for i in range(N):
            both = count(0, i) + count(1, i)
            for d in (0, 1):
                left(a_bufs[i], count(d, i), ring_send.at[kind, d, i])
                toward = (z == ZS - 2) if d == 0 else (z == 1)

                @pl.when(has_z[d] & jnp.logical_not(toward))
                def _():
                    left(b_bufs[i], count(d, i), z_send.at[kind, d, i])

                @pl.when(toward)
                def _():
                    left(b_bufs[i], both, z_send.at[kind, d, i])

    def gone_own(kind):
        for which in (0, 1):
            for i in range(N):
                left(bufs[which][i], 1, swap_send.at[kind, which, i])

    @pl.when(active)
    def _():
        gone(core)

        @pl.when(here)
        def _():
            gone_own(core)

    @pl.when(is_host)
    def _():
        gone(0)
        gone_own(0)
        for which in (0, 1):
            for i in range(N):
                left(bufs[which][i], 16, chip_send.at[which, i])

    @pl.when(plain)
    def _():
        for which in (0, 1):
            for i in range(N):
                left(bufs[which][i], 8, chip_send.at[which, i])

    for d in (0, 1):

        @pl.when(has_depth[d])
        def _():
            depth_copies[d].wait_send()

        @pl.when(has_row[d])
        def _():
            row_copies[d].wait_send()


def solution(mesh):
    def local(volume, weights):
        dma, regular = pltpu.SemaphoreType.DMA, pltpu.SemaphoreType.REGULAR
        return pl.pallas_call(
            kernel,
            out_shape=pltpu.VMEM(volume.shape, jnp.bfloat16),
            in_specs=[pl.BlockSpec(memory_space=pl.ANY)] * 2,
            out_specs=pl.BlockSpec(memory_space=pltpu.VMEM),
            scratch_shapes=[pltpu.VMEM((8, 2, 16, 256 * n), jnp.bfloat16) for n in PIECES]
            + [pltpu.VMEM((8, 2, 16, 256 * other_taps(i)), jnp.bfloat16) for i in range(N)]
            + [
                pltpu.VMEM((4, 4, 64, 256), jnp.bfloat16),
                pltpu.VMEM((3, 4, 4, 64, 256), jnp.bfloat16),
                pltpu.VMEM((256, 256), jnp.float32),
                dma((2, 2, N)),
                dma((2, 2, N)),
                dma((2, 2, N)),
                dma((2, 2, 4, N)),
                dma((2, 2, N)),
                dma((2, 2, 4, N)),
                dma((2, N)),
                dma((2, N)),
                dma((4,)),
                dma((4,)),
                dma(()),
                regular,
                regular,
                regular,
            ],
            compiler_params=pltpu.CompilerParams(collective_id=0, has_side_effects=True),
            name="conv_gather",
        )(volume, weights.T)

    return jax.shard_map(
        local,
        mesh=mesh,
        in_specs=(P("slab", "chan", None, None), P(None, "slab")),
        out_specs=P("slab", "chan", None, None),
        check_vma=False,
    )
```

```python
import jax
import jax.numpy as jnp
from jax import lax
from jax.experimental import pallas as pl
from jax.experimental.pallas import tpu as pltpu
from jax.sharding import PartitionSpec as P

MESH = pl.DeviceIdType.MESH
PIECES = (6, 4, 4)
N = len(PIECES)
LAST = N - 1
EDGE = (2,)
ZS = 12
LAG = 2


def first_tap(i, half):
    low = sum(PIECES[:i])
    high = 13 if i == LAST else 13 + PIECES[LAST] + low
    return low + half * (high - low)


def other_taps(i):
    return PIECES[i] - 1 if i == LAST else PIECES[i]


def hops(d, k, i):
    return k < 3 or (k == 3 and (i == 0) == (d == 0))


def count(d, i):
    return 3 + hops(d, 3, i)


def kernel(vol, w, out, *scratch):
    a_bufs, b_bufs = scratch[:N], scratch[N : 2 * N]
    (halo, shifted, acc, own, swap_send, ring_send, ring_recv, z_send, z_recv, edge_send,
     chip_send, chip_recv, halo_send, halo_recv, mid_sem, near_sem, far_sem, late_sem) = scratch[2 * N :]
    bufs = (a_bufs, b_bufs)
    s, ch = lax.axis_index("slab"), lax.axis_index("chan")
    y, xh = s // 2, s % 2
    core, xl, z = ch % 2, (ch // 2) % 2, ch // 4
    half = z % 2
    at_edge = (z == 0) | (z == ZS - 1)
    is_late = (s == 0) & (ch == 0)
    is_host = (s == 0) & (ch == 1)
    meets_late = (s == 1) & (ch == 0)
    active = jnp.logical_not(is_late)
    plain = jnp.logical_not((s == 0) & (ch < 2))
    here = core == xh

    def host(dev):
        return dev[0], jnp.where((dev[0] == 0) & (dev[1] == 0), 1, dev[1])

    def seat(kind):
        return ch - core + kind

    def ring_dev(d, kind):
        return host((lax.rem(s + (2 if d == 0 else 14), 16), seat(kind)))

    def swap_dev(kind):
        return host((s + 1 - 2 * xh, seat(kind) + 2 - 4 * xl))

    def z_dev(d, kind):
        c = seat(kind)
        return host((s, jnp.minimum(c + 4, 47) if d == 0 else jnp.maximum(c - 4, 0)))

    def devices(kind):
        return (
            (ring_dev(0, kind), ring_dev(1, kind)), swap_dev(kind),
            (z_dev(0, kind), z_dev(1, kind)), host((s, seat(kind) + 2 - 4 * xl)),
        )

    own_devices, zero_devices = devices(core), devices(0)

    def ring_of(kind):
        return (own_devices if kind is core else zero_devices)[0]

    def swap_of(kind):
        return (own_devices if kind is core else zero_devices)[1]

    def z_of(kind):
        return (own_devices if kind is core else zero_devices)[2]

    def across_of(kind):
        return (own_devices if kind is core else zero_devices)[3]

    partner = (s, ch + 1 - 2 * core)
    has_z = (z < ZS - 1, z > 0)
    depth_dev = ((jnp.minimum(s + 1, 15), ch), (jnp.maximum(s - 1, 0), ch))
    has_depth = (s < 15, s > 0)
    row_dev = ((s, jnp.minimum(ch + 1, 47)), (s, jnp.maximum(ch - 1, 0)))
    has_row = (ch < 47, ch > 0)

    def signal(sem, dev):
        pl.semaphore_signal(sem, inc=1, device_id=dev, device_id_type=MESH)

    def greet_as(sem, kind):
        for d in (0, 1):
            signal(sem, ring_of(kind)[d])
        signal(sem, swap_of(kind))
        signal(sem, across_of(kind))

    def greet(sem):
        greet_as(sem, core)

        @pl.when(plain)
        def _():
            signal(sem, partner)

        @pl.when(is_host)
        def _():
            greet_as(sem, 0)

    n_plane = jnp.where(is_host, 8, 5)
    n_z = has_z[0].astype(jnp.int32) + has_z[1].astype(jnp.int32)

    barrier = pltpu.get_barrier_semaphore()

    @pl.when(active)
    def _():
        greet(barrier)

    def greet_z(kind):
        for d in (0, 1):

            @pl.when(has_z[d])
            def _():
                signal(barrier, z_of(kind)[d])

    @pl.when(active)
    def _():
        greet_z(core)

    @pl.when(is_host)
    def _():
        greet_z(0)

    @pl.when(is_host | meets_late)
    def _():
        signal(barrier, (0, 0))

    pl.semaphore_wait(barrier, jnp.where(is_late, 2, n_plane + n_z * jnp.where(is_host, 2, 1)))

    @pl.when(is_late)
    def _():
        signal(late_sem, (0, 1))
        signal(late_sem, (1, 0))

    def remote(src, dst, send, recv, dev):
        return pltpu.make_async_remote_copy(
            src_ref=src, dst_ref=dst, send_sem=send, recv_sem=recv,
            device_id=dev, device_id_type=MESH,
        )

    def lanes(start, taps):
        return pl.ds(pl.multiple_of(start * 256, 256), taps * 256)

    def taps_of(which, i):
        if which == 0:
            return first_tap(i, half), PIECES[i]
        return first_tap(i, 1 - half) + ((1 - half) if i == LAST else 0), other_taps(i)

    def land(sem, ref):
        pltpu.make_async_copy(ref, ref, sem).wait()

    blocks = [[lax.rem(y + (7 - k if d == 0 else 1 + k), 8) for k in range(4)] for d in (0, 1)]

    def block_of(d, k):
        return y if k < 0 else blocks[d][k]

    def ring_copy(d, k, i, kind, src=None):
        ref = a_bufs[i].at[block_of(d, k - 1), kind]
        return remote(
            ref if src is None else src, ref,
            ring_send.at[kind, d, i], ring_recv.at[kind, d, k, i], ring_of(kind)[d],
        )

    def edge_copy(d, k, i, kind, src=None):
        ref = b_bufs[i].at[block_of(d, k - 1), kind]
        return remote(
            ref if src is None else src, ref,
            edge_send.at[kind, d, i], z_recv.at[kind, d, k, i], ring_of(kind)[d],
        )

    def edge_events(k, i, kind):
        @pl.when(at_edge)
        def _():
            for d in (0, 1):
                land(z_recv.at[kind, d, k, i], b_bufs[i].at[block_of(d, k), kind])
                if hops(d, k + 1, i):
                    edge_copy(d, k + 1, i, kind).start()

    def z_copy(d, k, i, to, kind):
        block = block_of(d, k)
        if i == LAST:
            src = a_bufs[i].at[block, kind, :, lanes(half, other_taps(i))]
        else:
            src = a_bufs[i].at[block, kind]
        return remote(
            src, b_bufs[i].at[block, kind],
            z_send.at[kind, to, i], z_recv.at[kind, d, k, i], z_of(kind)[to],
        )

    def chip_give(which, i):
        @pl.when(plain)
        def _():
            ref = bufs[which][i].at[:, core]
            remote(ref, ref, chip_send.at[which, i], chip_recv.at[which, i], partner).start()

    def host_give(which, i, early):
        for part in ((slice(0, 4), slice(5, 8)) if early else (slice(4, 5),)):
            ref = bufs[which][i].at[part]
            remote(ref, ref, chip_send.at[which, i], chip_recv.at[which, i], partner).start()

    def own_src(which, i):
        start, taps = taps_of(which, i)
        return w.at[:, lanes(start, taps)]

    def give_a(kind):
        for i in range(N):
            src, mine = own_src(0, i), a_bufs[i].at[y, kind]
            remote(src, mine, swap_send.at[kind, 0, i], own.at[kind, 0, i], swap_of(kind)).start()
            for d in (0, 1):
                ring_copy(d, 0, i, kind, src).start()

    def give_b(kind):
        for i in range(N):
            src, mine = own_src(1, i), b_bufs[i].at[y, kind]
            remote(src, mine, swap_send.at[kind, 1, i], own.at[kind, 1, i], swap_of(kind)).start()
            if i in EDGE:

                @pl.when(at_edge)
                def _():
                    for d in (0, 1):
                        edge_copy(d, 0, i, kind, src).start()

    def keep(kind):
        for which in (0, 1):
            for i in range(N):
                src, mine = own_src(which, i), bufs[which][i].at[y, kind]
                pltpu.make_async_copy(src, mine, own.at[kind, which, i]).start()

    def ring_events(k, i, kind):
        for d in (0, 1):
            if not hops(d, k, i):
                continue
            land(ring_recv.at[kind, d, k, i], a_bufs[i].at[block_of(d, k), kind])
            if hops(d, k + 1, i):
                ring_copy(d, k + 1, i, kind).start()
            away = (z == 1) if d == 0 else (z == ZS - 2)

            toward = (z == ZS - 2) if d == 0 else (z == 1)

            @pl.when(has_z[d] & jnp.logical_not(toward) if i in EDGE else has_z[d])
            def _():
                z_copy(d, k, i, d, kind).start()

            if i not in EDGE:

                @pl.when(away)
                def _():
                    z_copy(d, k, i, 1 - d, kind).start()

    def z_events(k, i, kind):
        for d in (0, 1):
            if not hops(d, k, i):
                continue
            if i in EDGE and k < 3:

                @pl.when(jnp.logical_not(at_edge))
                def _():
                    land(z_recv.at[kind, d, k, i], b_bufs[i].at[block_of(d, k), kind])

            else:
                land(z_recv.at[kind, d, k, i], b_bufs[i].at[block_of(d, k), kind])

    depth_copies = [
        remote(vol.at[1:2], halo.at[0:1, 1:3], halo_send.at[0], halo_recv.at[0], depth_dev[0]),
        remote(vol.at[0:1], halo.at[3:4, 1:3], halo_send.at[1], halo_recv.at[1], depth_dev[1]),
    ]
    row_copies = [
        remote(halo.at[:, 2:3], halo.at[:, 0:1], halo_send.at[2], halo_recv.at[2], row_dev[0]),
        remote(halo.at[:, 1:2], halo.at[:, 3:4], halo_send.at[3], halo_recv.at[3], row_dev[1]),
    ]

    late_row = remote(
        halo.at[1:3, 2:3], halo.at[1:3, 0:1], halo_send.at[2], halo_recv.at[2], row_dev[0]
    )
    corner = remote(
        vol.at[0:1, 1:2], halo.at[3:4, 0:1], halo_send.at[4], halo_recv.at[4], (0, 1)
    )

    def halo_rows():
        for d in (0, 1):

            @pl.when(has_depth[1 - d])
            def _():
                depth_copies[d].wait_recv()

        land(mid_sem, halo.at[1:3, 1:3])
        for d in (0, 1):
            wanted = has_row[d] if d == 0 else has_row[d] & jnp.logical_not(is_host)

            @pl.when(wanted)
            def _():
                row_copies[d].start()

    def spread(d):
        for r in range(4):
            there = []
            if d == 0:
                there.append(s > 0)
            if d == 3:
                there.append(s < 15)
            if r == 0:
                there.append(ch > 0)
            if r == 3:
                there.append(ch < 47)
            x = halo[d, r].astype(jnp.float32)
            for cond in there:
                x = jnp.where(cond, x, 0.0)
            at = lax.broadcasted_iota(jnp.int32, x.shape, 0)
            low = jnp.where(at == 0, 0.0, pltpu.roll(x, 1, 0))
            high = jnp.where(at == 63, 0.0, pltpu.roll(x, 63, 0))
            shifted[0, d, r] = low.astype(jnp.bfloat16)
            shifted[1, d, r] = x.astype(jnp.bfloat16)
            shifted[2, d, r] = high.astype(jnp.bfloat16)

    def multiply(which, i):
        buf = bufs[which][i]

        @pl.when(plain)
        def _():
            land(chip_recv.at[which, i], buf.at[:, core])

        @pl.when(is_late)
        def _():
            land(chip_recv.at[which, i], buf)

        start, number = taps_of(which, i)
        taps = []
        for j in range(number):
            t = start + j
            a, b, e = t // 9, (t // 3) % 3, t % 3
            taps.append(
                jnp.concatenate(
                    [shifted[e, a + dd, b + rr] for dd in (0, 1) for rr in (0, 1)], axis=0
                )
            )
        left = jnp.concatenate(taps, axis=1)
        part = lax.dot_general(
            left, buf[...].reshape(256, 256 * number), (((1,), (1,)), ((), ())), preferred_element_type=jnp.float32
        )
        if which == 0 and i == 0:
            acc[...] = part
        else:
            acc[...] += part

    pltpu.make_async_copy(vol, halo.at[1:3, 1:3], mid_sem).start()

    @pl.when(is_late)
    def _():
        depth_copies[0].start()
        land(mid_sem, halo.at[1:3, 1:3])
        late_row.start()

    @pl.when(active)
    def _():
        greet(near_sem)

        @pl.when(is_host)
        def _():
            give_a(0)

        @pl.when(here)
        def _():
            give_a(core)
            give_b(core)
            keep(core)

        @pl.when(is_host)
        def _():
            give_b(0)
            keep(0)

        @pl.when(jnp.logical_not(here))
        def _():
            for i in range(N):
                land(own.at[core, 0, i], a_bufs[i].at[y, core])
                for d in (0, 1):
                    ring_copy(d, 0, i, core, a_bufs[i].at[y, core]).start()

        pl.semaphore_wait(near_sem, n_plane)
        greet(far_sem)
        for k in range(4):
            for i in range(N):
                ring_events(k, i, core)
                if k > 0 and i in EDGE:
                    edge_events(k - 1, i, core)

                @pl.when(is_host)
                def _():
                    ring_events(k, i, 0)
                    if k > 0 and i in EDGE:
                        edge_events(k - 1, i, 0)

                if k == 3:

                    @pl.when(plain)
                    def _():
                        chip_give(0, i)

                if k >= LAG:
                    z_events(k - LAG, i, core)
            if k == 0:
                pl.semaphore_wait(far_sem, n_plane)
                for d in (0, 1):
                    wanted = has_depth[d] if d == 0 else has_depth[d] & jnp.logical_not(meets_late)

                    @pl.when(wanted)
                    def _():
                        depth_copies[d].start()

                @pl.when(meets_late)
                def _():
                    corner.start()

                @pl.when(here)
                def _():
                    for which in (0, 1):
                        for i in range(N):
                            land(own.at[core, which, i], bufs[which][i].at[y, core])

                @pl.when(jnp.logical_not(here))
                def _():
                    for i in range(N):
                        land(own.at[core, 1, i], b_bufs[i].at[y, core])
                        if i in EDGE:

                            @pl.when(at_edge)
                            def _():
                                for d in (0, 1):
                                    edge_copy(d, 0, i, core).start()

            if k == 2:

                @pl.when(meets_late)
                def _():
                    pl.semaphore_wait(late_sem, 1)
                    depth_copies[1].start()

                halo_rows()

                @pl.when(is_host)
                def _():
                    pl.semaphore_wait(late_sem, 1)
                    row_copies[1].start()
                    for which in (0, 1):
                        for i in range(N):
                            land(own.at[0, which, i], bufs[which][i].at[y, 0])
                    for i in range(N):
                        host_give(0, i, True)

        @pl.when(is_host)
        def _():
            for i in range(N):
                host_give(0, i, False)

        for k in range(4 - LAG, 3):
            for i in range(N):
                z_events(k, i, core)

        @pl.when(is_host)
        def _():
            for i in range(N):
                for k in range(3):
                    z_events(k, i, 0)
                host_give(1, i, True)

    for d in (0, 1):

        @pl.when(has_row[1 - d] & jnp.logical_not(is_host) if d == 0 else has_row[1 - d])
        def _():
            row_copies[d].wait_recv()

    @pl.when(is_host)
    def _():
        late_row.wait_recv()
        corner.wait_recv()

    @pl.when(is_late)
    def _():
        depth_copies[1].wait_recv()

    for d in range(4):
        spread(d)
    for i in range(N):
        multiply(0, i)

        @pl.when(active)
        def _():
            z_events(3, i, core)

        @pl.when(is_host)
        def _():
            z_events(3, i, 0)
            host_give(1, i, False)

        chip_give(1, i)

    for i in range(N):
        multiply(1, i)
    out[...] = acc[...].astype(jnp.bfloat16).reshape(out.shape)

    def left(buf, blocks, sem):
        land(sem, buf if blocks == 16 else buf.at[0:blocks, 0])

    def gone(kind):
        for i in range(N):
            both = count(0, i) + count(1, i)
            for d in (0, 1):
                left(a_bufs[i], count(d, i), ring_send.at[kind, d, i])
                toward = (z == ZS - 2) if d == 0 else (z == 1)

                @pl.when(has_z[d] & jnp.logical_not(toward))
                def _():
                    left(b_bufs[i], count(d, i), z_send.at[kind, d, i])

                if i in EDGE:

                    @pl.when(at_edge)
                    def _():
                        left(b_bufs[i], count(d, i), edge_send.at[kind, d, i])

                else:

                    @pl.when(toward)
                    def _():
                        left(b_bufs[i], both, z_send.at[kind, d, i])

    def gone_own(kind):
        for which in (0, 1):
            for i in range(N):
                left(bufs[which][i], 1, swap_send.at[kind, which, i])

    @pl.when(active)
    def _():
        gone(core)

        @pl.when(here)
        def _():
            gone_own(core)

    @pl.when(is_host)
    def _():
        gone(0)
        gone_own(0)
        for which in (0, 1):
            for i in range(N):
                left(bufs[which][i], 16, chip_send.at[which, i])

    @pl.when(plain)
    def _():
        for which in (0, 1):
            for i in range(N):
                left(bufs[which][i], 8, chip_send.at[which, i])

    for d in (0, 1):

        @pl.when(has_depth[d])
        def _():
            depth_copies[d].wait_send()

        @pl.when(has_row[d] & active if d == 0 else has_row[d])
        def _():
            row_copies[d].wait_send()

    @pl.when(is_late)
    def _():
        late_row.wait_send()

    @pl.when(meets_late)
    def _():
        corner.wait_send()


def solution(mesh):
    def local(volume, weights):
        dma, regular = pltpu.SemaphoreType.DMA, pltpu.SemaphoreType.REGULAR
        return pl.pallas_call(
            kernel,
            out_shape=pltpu.VMEM(volume.shape, jnp.bfloat16),
            in_specs=[pl.BlockSpec(memory_space=pl.ANY)] * 2,
            out_specs=pl.BlockSpec(memory_space=pltpu.VMEM),
            scratch_shapes=[pltpu.VMEM((8, 2, 16, 256 * n), jnp.bfloat16) for n in PIECES]
            + [pltpu.VMEM((8, 2, 16, 256 * other_taps(i)), jnp.bfloat16) for i in range(N)]
            + [
                pltpu.VMEM((4, 4, 64, 256), jnp.bfloat16),
                pltpu.VMEM((3, 4, 4, 64, 256), jnp.bfloat16),
                pltpu.VMEM((256, 256), jnp.float32),
                dma((2, 2, N)),
                dma((2, 2, N)),
                dma((2, 2, N)),
                dma((2, 2, 4, N)),
                dma((2, 2, N)),
                dma((2, 2, 4, N)),
                dma((2, 2, N)),
                dma((2, N)),
                dma((2, N)),
                dma((5,)),
                dma((5,)),
                dma(()),
                regular,
                regular,
                regular,
            ],
            compiler_params=pltpu.CompilerParams(collective_id=0, has_side_effects=True),
            name="conv_gather",
        )(volume, weights.T)

    return jax.shard_map(
        local,
        mesh=mesh,
        in_specs=(P("slab", "chan", None, None), P(None, "slab")),
        out_specs=P("slab", "chan", None, None),
        check_vma=False,
    )
```

```python
import jax
import jax.numpy as jnp
from jax import lax
from jax.experimental import pallas as pl
from jax.experimental.pallas import tpu as pltpu
from jax.sharding import PartitionSpec as P

MESH = pl.DeviceIdType.MESH
PIECES = (6, 4, 4)
N = len(PIECES)
LAST = N - 1
EDGE = (2,)
ZS = 12
LAG = 2


def first_tap(i, half):
    low = sum(PIECES[:i])
    high = 13 if i == LAST else 13 + PIECES[LAST] + low
    return low + half * (high - low)


def other_taps(i):
    return PIECES[i] - 1 if i == LAST else PIECES[i]


def hops(d, k, i):
    return k < 3 or (k == 3 and (i == 0) == (d == 0))


def count(d, i):
    return 3 + hops(d, 3, i)


def kernel(vol, w, out, *scratch):
    a_bufs, b_bufs = scratch[:N], scratch[N : 2 * N]
    (halo, shifted, acc, own, swap_send, ring_send, ring_recv, z_send, z_recv, edge_send,
     chip_send, chip_recv, halo_send, halo_recv, mid_sem, near_sem, far_sem, late_sem) = scratch[2 * N :]
    bufs = (a_bufs, b_bufs)
    s, ch = lax.axis_index("slab"), lax.axis_index("chan")
    y, xh = s // 2, s % 2
    core, xl, z = ch % 2, (ch // 2) % 2, ch // 4
    half = z % 2
    at_edge = (z == 0) | (z == ZS - 1)
    is_late = (s == 0) & (ch == 0)
    is_host = (s == 0) & (ch == 1)
    meets_late = (s == 1) & (ch == 0)
    active = jnp.logical_not(is_late)
    plain = jnp.logical_not((s == 0) & (ch < 2))
    here = core == xh

    def host(dev):
        return dev[0], jnp.where((dev[0] == 0) & (dev[1] == 0), 1, dev[1])

    def seat(kind):
        return ch - core + kind

    def ring_dev(d, kind):
        return host((lax.rem(s + (2 if d == 0 else 14), 16), seat(kind)))

    def swap_dev(kind):
        return host((s + 1 - 2 * xh, seat(kind) + 2 - 4 * xl))

    def z_dev(d, kind):
        c = seat(kind)
        return host((s, jnp.minimum(c + 4, 47) if d == 0 else jnp.maximum(c - 4, 0)))

    def devices(kind):
        return (
            (ring_dev(0, kind), ring_dev(1, kind)), swap_dev(kind),
            (z_dev(0, kind), z_dev(1, kind)), host((s, seat(kind) + 2 - 4 * xl)),
        )

    own_devices, zero_devices = devices(core), devices(0)

    def ring_of(kind):
        return (own_devices if kind is core else zero_devices)[0]

    def swap_of(kind):
        return (own_devices if kind is core else zero_devices)[1]

    def z_of(kind):
        return (own_devices if kind is core else zero_devices)[2]

    def across_of(kind):
        return (own_devices if kind is core else zero_devices)[3]

    def slot(kind):
        return 0 if kind is core else 1

    def guest(dev):
        return ((core == 0) & (dev[0] == 0) & (dev[1] == 1)).astype(jnp.int32)

    ring_guest = [guest(own_devices[0][d]) for d in (0, 1)]
    z_guest = guest(own_devices[2][1])

    def ring_slot(d, kind):
        return ring_guest[d] if kind is core else 0

    def z_slot(to, kind):
        return z_guest if kind is core and to == 1 else 0

    partner = (s, ch + 1 - 2 * core)
    has_z = (z < ZS - 1, z > 0)
    depth_dev = ((jnp.minimum(s + 1, 15), ch), (jnp.maximum(s - 1, 0), ch))
    has_depth = (s < 15, s > 0)
    row_dev = ((s, jnp.minimum(ch + 1, 47)), (s, jnp.maximum(ch - 1, 0)))
    has_row = (ch < 47, ch > 0)

    def signal(sem, dev):
        pl.semaphore_signal(sem, inc=1, device_id=dev, device_id_type=MESH)

    def greet_as(sem, kind):
        for d in (0, 1):
            signal(sem, ring_of(kind)[d])
        signal(sem, swap_of(kind))
        signal(sem, across_of(kind))

    def greet(sem):
        greet_as(sem, core)

        @pl.when(plain)
        def _():
            signal(sem, partner)

        @pl.when(is_host)
        def _():
            greet_as(sem, 0)

    n_plane = jnp.where(is_host, 8, 5)
    n_z = has_z[0].astype(jnp.int32) + has_z[1].astype(jnp.int32)

    barrier = pltpu.get_barrier_semaphore()

    @pl.when(active)
    def _():
        greet(barrier)

    def greet_z(kind):
        for d in (0, 1):

            @pl.when(has_z[d])
            def _():
                signal(barrier, z_of(kind)[d])

    @pl.when(active)
    def _():
        greet_z(core)

    @pl.when(is_host)
    def _():
        greet_z(0)

    @pl.when(is_host | meets_late)
    def _():
        signal(barrier, (0, 0))

    pl.semaphore_wait(barrier, jnp.where(is_late, 2, n_plane + n_z * jnp.where(is_host, 2, 1)))

    @pl.when(is_late)
    def _():
        signal(late_sem, (0, 1))
        signal(late_sem, (1, 0))

    def remote(src, dst, send, recv, dev):
        return pltpu.make_async_remote_copy(
            src_ref=src, dst_ref=dst, send_sem=send, recv_sem=recv,
            device_id=dev, device_id_type=MESH,
        )

    def lanes(start, taps):
        return pl.ds(pl.multiple_of(start * 256, 256), taps * 256)

    def taps_of(which, i):
        if which == 0:
            return first_tap(i, half), PIECES[i]
        return first_tap(i, 1 - half) + ((1 - half) if i == LAST else 0), other_taps(i)

    def land(sem, ref):
        pltpu.make_async_copy(ref, ref, sem).wait()

    blocks = [[lax.rem(y + (7 - k if d == 0 else 1 + k), 8) for k in range(4)] for d in (0, 1)]

    def block_of(d, k):
        return y if k < 0 else blocks[d][k]

    def ring_copy(d, k, i, kind, src=None):
        ref = a_bufs[i].at[block_of(d, k - 1), kind]
        return remote(
            ref if src is None else src, ref,
            ring_send.at[slot(kind), d, i], ring_recv.at[ring_slot(d, kind), d, k, i], ring_of(kind)[d],
        )

    def edge_copy(d, k, i, kind, src=None):
        ref = b_bufs[i].at[block_of(d, k - 1), kind]
        return remote(
            ref if src is None else src, ref,
            edge_send.at[slot(kind), d, i], z_recv.at[ring_slot(d, kind), d, k, i], ring_of(kind)[d],
        )

    def edge_events(k, i, kind):
        @pl.when(at_edge)
        def _():
            for d in (0, 1):
                land(z_recv.at[slot(kind), d, k, i], b_bufs[i].at[block_of(d, k), kind])
                if hops(d, k + 1, i):
                    edge_copy(d, k + 1, i, kind).start()

    def z_copy(d, k, i, to, kind):
        block = block_of(d, k)
        if i == LAST:
            src = a_bufs[i].at[block, kind, :, lanes(half, other_taps(i))]
        else:
            src = a_bufs[i].at[block, kind]
        return remote(
            src, b_bufs[i].at[block, kind],
            z_send.at[slot(kind), to, i], z_recv.at[z_slot(to, kind), d, k, i], z_of(kind)[to],
        )

    def chip_give(which, i):
        @pl.when(plain)
        def _():
            ref = bufs[which][i].at[:, core]
            remote(ref, ref, chip_send.at[which, i], chip_recv.at[which, i], partner).start()

    def host_give(which, i, early):
        for part in ((slice(0, 4), slice(5, 8)) if early else (slice(4, 5),)):
            ref = bufs[which][i].at[part]
            remote(ref, ref, chip_send.at[which, i], chip_recv.at[which, i], partner).start()

    def own_src(which, i):
        start, taps = taps_of(which, i)
        return w.at[:, lanes(start, taps)]

    def give_a(kind):
        for i in range(N):
            src, mine = own_src(0, i), a_bufs[i].at[y, kind]
            remote(src, mine, swap_send.at[slot(kind), 0, i], own.at[0, 0, i], swap_of(kind)).start()
            for d in (0, 1):
                ring_copy(d, 0, i, kind, src).start()

    def give_b(kind):
        for i in range(N):
            src, mine = own_src(1, i), b_bufs[i].at[y, kind]
            remote(src, mine, swap_send.at[slot(kind), 1, i], own.at[0, 1, i], swap_of(kind)).start()
            if i in EDGE:

                @pl.when(at_edge)
                def _():
                    for d in (0, 1):
                        edge_copy(d, 0, i, kind, src).start()

    def keep(kind):
        for which in (0, 1):
            for i in range(N):
                src, mine = own_src(which, i), bufs[which][i].at[y, kind]
                pltpu.make_async_copy(src, mine, own.at[slot(kind), which, i]).start()

    def ring_events(k, i, kind):
        for d in (0, 1):
            if not hops(d, k, i):
                continue
            land(ring_recv.at[slot(kind), d, k, i], a_bufs[i].at[block_of(d, k), kind])
            if hops(d, k + 1, i):
                ring_copy(d, k + 1, i, kind).start()
        for d in (0, 1):
            if not hops(d, k, i):
                continue
            away = (z == 1) if d == 0 else (z == ZS - 2)

            toward = (z == ZS - 2) if d == 0 else (z == 1)

            @pl.when(has_z[d] & jnp.logical_not(toward) if i in EDGE else has_z[d])
            def _():
                z_copy(d, k, i, d, kind).start()

            if i not in EDGE:

                @pl.when(away)
                def _():
                    z_copy(d, k, i, 1 - d, kind).start()

    def z_events(k, i, kind):
        for d in (0, 1):
            if not hops(d, k, i):
                continue
            if i in EDGE and k < 3:

                @pl.when(jnp.logical_not(at_edge))
                def _():
                    land(z_recv.at[slot(kind), d, k, i], b_bufs[i].at[block_of(d, k), kind])

            else:
                land(z_recv.at[slot(kind), d, k, i], b_bufs[i].at[block_of(d, k), kind])

    depth_copies = [
        remote(vol.at[1:2], halo.at[0:1, 1:3], halo_send.at[0], halo_recv.at[0], depth_dev[0]),
        remote(vol.at[0:1], halo.at[3:4, 1:3], halo_send.at[1], halo_recv.at[1], depth_dev[1]),
    ]
    row_copies = [
        remote(halo.at[:, 2:3], halo.at[:, 0:1], halo_send.at[2], halo_recv.at[2], row_dev[0]),
        remote(halo.at[:, 1:2], halo.at[:, 3:4], halo_send.at[3], halo_recv.at[3], row_dev[1]),
    ]

    late_row = remote(
        halo.at[1:3, 2:3], halo.at[1:3, 0:1], halo_send.at[2], halo_recv.at[2], row_dev[0]
    )
    corner = remote(
        vol.at[0:1, 1:2], halo.at[3:4, 0:1], halo_send.at[4], halo_recv.at[4], (0, 1)
    )

    def halo_rows():
        for d in (0, 1):

            @pl.when(has_depth[1 - d])
            def _():
                depth_copies[d].wait_recv()

        land(mid_sem, halo.at[1:3, 1:3])
        for d in (0, 1):
            wanted = has_row[d] if d == 0 else has_row[d] & jnp.logical_not(is_host)

            @pl.when(wanted)
            def _():
                row_copies[d].start()

    def spread(d):
        for r in range(4):
            there = []
            if d == 0:
                there.append(s > 0)
            if d == 3:
                there.append(s < 15)
            if r == 0:
                there.append(ch > 0)
            if r == 3:
                there.append(ch < 47)
            x = halo[d, r].astype(jnp.float32)
            for cond in there:
                x = jnp.where(cond, x, 0.0)
            at = lax.broadcasted_iota(jnp.int32, x.shape, 0)
            low = jnp.where(at == 0, 0.0, pltpu.roll(x, 1, 0))
            high = jnp.where(at == 63, 0.0, pltpu.roll(x, 63, 0))
            shifted[0, d, r] = low.astype(jnp.bfloat16)
            shifted[1, d, r] = x.astype(jnp.bfloat16)
            shifted[2, d, r] = high.astype(jnp.bfloat16)

    def multiply(which, i):
        buf = bufs[which][i]

        @pl.when(plain)
        def _():
            land(chip_recv.at[which, i], buf.at[:, core])

        @pl.when(is_late)
        def _():
            land(chip_recv.at[which, i], buf)

        start, number = taps_of(which, i)
        taps = []
        for j in range(number):
            t = start + j
            a, b, e = t // 9, (t // 3) % 3, t % 3
            taps.append(
                jnp.concatenate(
                    [shifted[e, a + dd, b + rr] for dd in (0, 1) for rr in (0, 1)], axis=0
                )
            )
        left = jnp.concatenate(taps, axis=1)
        part = lax.dot_general(
            left, buf[...].reshape(256, 256 * number), (((1,), (1,)), ((), ())), preferred_element_type=jnp.float32
        )
        if which == 0 and i == 0:
            acc[...] = part
        else:
            acc[...] += part

    pltpu.make_async_copy(vol, halo.at[1:3, 1:3], mid_sem).start()

    @pl.when(is_late)
    def _():
        depth_copies[0].start()
        land(mid_sem, halo.at[1:3, 1:3])
        late_row.start()

    @pl.when(active)
    def _():
        greet(near_sem)

        @pl.when(is_host)
        def _():
            give_a(0)

        @pl.when(here)
        def _():
            give_a(core)
            give_b(core)
            keep(core)

        @pl.when(is_host)
        def _():
            give_b(0)
            keep(0)

        @pl.when(jnp.logical_not(here))
        def _():
            for i in range(N):
                land(own.at[0, 0, i], a_bufs[i].at[y, core])
                for d in (0, 1):
                    ring_copy(d, 0, i, core, a_bufs[i].at[y, core]).start()

        pl.semaphore_wait(near_sem, n_plane)
        greet(far_sem)
        for k in range(4):
            for i in range(N):
                ring_events(k, i, core)
                if k > 0 and i in EDGE:
                    edge_events(k - 1, i, core)

                @pl.when(is_host)
                def _():
                    ring_events(k, i, 0)
                    if k > 0 and i in EDGE:
                        edge_events(k - 1, i, 0)

                if k == 3:

                    @pl.when(plain)
                    def _():
                        chip_give(0, i)

                if k >= LAG:
                    z_events(k - LAG, i, core)
            if k == 0:
                pl.semaphore_wait(far_sem, n_plane)
                for d in (0, 1):
                    wanted = has_depth[d] if d == 0 else has_depth[d] & jnp.logical_not(meets_late)

                    @pl.when(wanted)
                    def _():
                        depth_copies[d].start()

                @pl.when(meets_late)
                def _():
                    corner.start()

                @pl.when(here)
                def _():
                    for which in (0, 1):
                        for i in range(N):
                            land(own.at[0, which, i], bufs[which][i].at[y, core])

                @pl.when(jnp.logical_not(here))
                def _():
                    for i in range(N):
                        land(own.at[0, 1, i], b_bufs[i].at[y, core])
                        if i in EDGE:

                            @pl.when(at_edge)
                            def _():
                                for d in (0, 1):
                                    edge_copy(d, 0, i, core).start()

            if k == 2:

                @pl.when(meets_late)
                def _():
                    pl.semaphore_wait(late_sem, 1)
                    depth_copies[1].start()

                halo_rows()

                @pl.when(is_host)
                def _():
                    pl.semaphore_wait(late_sem, 1)
                    row_copies[1].start()
                    for which in (0, 1):
                        for i in range(N):
                            land(own.at[1, which, i], bufs[which][i].at[y, 0])
                    for i in range(N):
                        host_give(0, i, True)

        @pl.when(is_host)
        def _():
            for i in range(N):
                host_give(0, i, False)

        for k in range(4 - LAG, 3):
            for i in range(N):
                z_events(k, i, core)

        @pl.when(is_host)
        def _():
            for i in range(N):
                for k in range(3):
                    z_events(k, i, 0)
                host_give(1, i, True)

    for d in (0, 1):

        @pl.when(has_row[1 - d] & jnp.logical_not(is_host) if d == 0 else has_row[1 - d])
        def _():
            row_copies[d].wait_recv()

    @pl.when(is_host)
    def _():
        late_row.wait_recv()
        corner.wait_recv()

    @pl.when(is_late)
    def _():
        depth_copies[1].wait_recv()

    for d in range(4):
        spread(d)
    for i in range(N):
        multiply(0, i)

        @pl.when(active)
        def _():
            z_events(3, i, core)

        @pl.when(is_host)
        def _():
            z_events(3, i, 0)
            host_give(1, i, False)

        chip_give(1, i)

    for i in range(N):
        multiply(1, i)
    out[...] = acc[...].astype(jnp.bfloat16).reshape(out.shape)

    def left(buf, blocks, sem):
        land(sem, buf if blocks == 16 else buf.at[0:blocks, 0])

    def gone(kind):
        for i in range(N):
            both = count(0, i) + count(1, i)
            for d in (0, 1):
                left(a_bufs[i], count(d, i), ring_send.at[slot(kind), d, i])
                toward = (z == ZS - 2) if d == 0 else (z == 1)

                @pl.when(has_z[d] & jnp.logical_not(toward))
                def _():
                    left(b_bufs[i], count(d, i), z_send.at[slot(kind), d, i])

                if i in EDGE:

                    @pl.when(at_edge)
                    def _():
                        left(b_bufs[i], count(d, i), edge_send.at[slot(kind), d, i])

                else:

                    @pl.when(toward)
                    def _():
                        left(b_bufs[i], both, z_send.at[slot(kind), d, i])

    def gone_own(kind):
        for which in (0, 1):
            for i in range(N):
                left(bufs[which][i], 1, swap_send.at[slot(kind), which, i])

    @pl.when(active)
    def _():
        gone(core)

        @pl.when(here)
        def _():
            gone_own(core)

    @pl.when(is_host)
    def _():
        gone(0)
        gone_own(0)
        for which in (0, 1):
            for i in range(N):
                left(bufs[which][i], 16, chip_send.at[which, i])

    @pl.when(plain)
    def _():
        for which in (0, 1):
            for i in range(N):
                left(bufs[which][i], 8, chip_send.at[which, i])

    for d in (0, 1):

        @pl.when(has_depth[d])
        def _():
            depth_copies[d].wait_send()

        @pl.when(has_row[d] & active if d == 0 else has_row[d])
        def _():
            row_copies[d].wait_send()

    @pl.when(is_late)
    def _():
        late_row.wait_send()

    @pl.when(meets_late)
    def _():
        corner.wait_send()


def solution(mesh):
    def local(volume, weights):
        dma, regular = pltpu.SemaphoreType.DMA, pltpu.SemaphoreType.REGULAR
        return pl.pallas_call(
            kernel,
            out_shape=pltpu.VMEM(volume.shape, jnp.bfloat16),
            in_specs=[pl.BlockSpec(memory_space=pl.ANY)] * 2,
            out_specs=pl.BlockSpec(memory_space=pltpu.VMEM),
            scratch_shapes=[pltpu.VMEM((8, 2, 16, 256 * n), jnp.bfloat16) for n in PIECES]
            + [pltpu.VMEM((8, 2, 16, 256 * other_taps(i)), jnp.bfloat16) for i in range(N)]
            + [
                pltpu.VMEM((4, 4, 64, 256), jnp.bfloat16),
                pltpu.VMEM((3, 4, 4, 64, 256), jnp.bfloat16),
                pltpu.VMEM((256, 256), jnp.float32),
                dma((2, 2, N)),
                dma((2, 2, N)),
                dma((2, 2, N)),
                dma((2, 2, 4, N)),
                dma((2, 2, N)),
                dma((2, 2, 4, N)),
                dma((2, 2, N)),
                dma((2, N)),
                dma((2, N)),
                dma((5,)),
                dma((5,)),
                dma(()),
                regular,
                regular,
                regular,
            ],
            compiler_params=pltpu.CompilerParams(collective_id=0, has_side_effects=True),
            name="conv_gather",
        )(volume, weights.T)

    return jax.shard_map(
        local,
        mesh=mesh,
        in_specs=(P("slab", "chan", None, None), P(None, "slab")),
        out_specs=P("slab", "chan", None, None),
        check_vma=False,
    )
```
